32 devices in a mesh: rows: 16 (over z, y, x), trees: 2 (over core).
Axes of the slice: x: 2, y: 2, z: 4, core: 2. Of those that a mesh axis runs over, the one named last changes fastest.
Arguments:
- tiles: bfloat16 [2, 16, 4, 256, 256], P('trees', 'rows'), may hold values from -0.0625 to 0.0625
- tile_src: int32 [2, 16, 4], P('trees', 'rows'), may hold values from 0 to 3, as said below
- tile_dst: int32 [2, 16, 4], P('trees', 'rows'), may hold values from 0 to 1
- leaf_rhs: bfloat16 [2, 16, 256, 128], P('trees', 'rows'), may hold values from -6 to 6
- leaf_inv: bfloat16 [2, 16, 256, 256], P('trees', 'rows'), may hold values from -0.375 to 0.375
- leaf_owner: int32 [2, 2], P('trees'), may hold values from 0 to 15, as said below
- anc_rhs: bfloat16 [2, 16, 256, 128], P('trees', 'rows'), may hold values from -5 to 5
- anc_inv: bfloat16 [16, 256, 256], P('rows'), may hold values from -0.25 to 0.25
- anc_owner: int32 [4], replicated, may hold values from 0 to 15, as said below
Outputs:
- solved: bfloat16 [4, 256, 128], P(None, None, 'rows')
The draws below stay inside these ranges and needn't reach their ends.
Inputs may be any that keep to these rules, and one draw needn't show every extreme that they name: `leaf_owner`: the 2 owners of one subtree differ. `anc_owner`: all owners differ. `tile_src`: a tile of wave w names a block below 2 * w.
All inputs are finite; a program needn't handle non-finite values.
Results may differ from the reference program's by a relative error of at most 0.011.
Values may be sent and summed in bfloat16 or wider, within the bound.
A program may use at most 64 MiB of HBM per device.

```python
import jax
import jax.numpy as jnp
from jax import lax

B = 256
R = 128
WAVES = 3
WB = 2
TW = 2
TILES = 4
ANC = 4
N_ROWS = 16
N_TREES = 2


def owner_list(key, count):
    order = jax.random.permutation(key, N_ROWS).astype(jnp.int32)
    place = jnp.argmax(order == N_ROWS - 1)
    return jnp.roll(order, -place)[:count]


def draw_leaf_owner(key, part):
    keys = jax.random.split(jax.random.fold_in(key, 11), N_TREES)
    return jax.vmap(lambda k: owner_list(k, WB))(keys)


def draw_anc_owner(key, part):
    return owner_list(jax.random.fold_in(key, 12), ANC)


def draw_tile_src(key, part):
    waves = jnp.arange(TILES, dtype=jnp.int32) // TW + 1
    limit = jnp.broadcast_to(WB * waves, (N_TREES, N_ROWS, TILES))
    values = jax.random.randint(jax.random.fold_in(key, 13), (N_TREES, N_ROWS, TILES), 0, limit).astype(jnp.int32)
    values = values.at[0, 0, 0].set(0)
    return values.at[0, 0, TILES - 1].set(WB * (WAVES - 1) - 1)


def draw_tile_dst(key, part):
    values = jax.random.randint(jax.random.fold_in(key, 14), (N_TREES, N_ROWS, TILES), 0, WB).astype(jnp.int32)
    values = values.at[0, 0, 0].set(0)
    return values.at[0, 0, TILES - 1].set(WB - 1)


def level_of(stream_key, shape, pieces, least, largest):
    def one(dim, shards_of):
        draws = jax.random.uniform(jax.random.fold_in(jax.random.fold_in(stream_key, 6), dim), (shards_of,), jnp.float32, least / len(pieces), largest / len(pieces))
        return jnp.repeat(jnp.exp(draws), shape[dim] // shards_of).reshape((-1,) + (1,) * (len(shape) - dim - 1))

    loudness = one(*pieces[0])
    for cut in pieces[1:]:
        loudness = loudness * one(*cut)
    return loudness


def normal_values(rng, dims, spread, reach, shards=(), kind=jnp.bfloat16):
    result = spread * jax.random.normal(rng, dims, jnp.float32)
    if shards:
        result = result * level_of(rng, dims, shards, -0.22, 0.18)
    return jnp.clip(result, -reach, reach).astype(kind)


def setup_inputs(seed: int = 0) -> dict:
    key_of = jax.random.split(jax.random.key(seed), 10)
    tiles = normal_values(key_of[0], (N_TREES, N_ROWS, TILES, B, B), (B * N_TREES * N_ROWS * TW // WB) ** -0.5, 0.0625, ((0, 2), (1, 16)))
    tile_src = draw_tile_src(jax.random.fold_in(key_of[9], 71), 0)
    tile_dst = draw_tile_dst(jax.random.fold_in(key_of[9], 71), 0)
    leaf_rhs = normal_values(key_of[3], (N_TREES, N_ROWS, B, R), 1.0, 6.0, ((0, 2), (1, 16)))
    leaf_inv = normal_values(key_of[4], (N_TREES, N_ROWS, B, B), B ** -0.5, 0.375, ((0, 2), (1, 16)))
    leaf_owner = draw_leaf_owner(jax.random.fold_in(key_of[9], 71), 0)
    anc_rhs = normal_values(key_of[6], (N_TREES, N_ROWS, B, R), 0.35, 5.0, ((0, 2), (1, 16)))
    anc_inv = normal_values(key_of[7], (N_ROWS, B, B), (2 * B) ** -0.5, 0.25, ((0, 16),))
    anc_owner = draw_anc_owner(jax.random.fold_in(key_of[9], 71), 0)
    return dict(tiles=tiles, tile_src=tile_src, tile_dst=tile_dst, leaf_rhs=leaf_rhs, leaf_inv=leaf_inv, leaf_owner=leaf_owner, anc_rhs=anc_rhs, anc_inv=anc_inv, anc_owner=anc_owner)


def reference(tiles, tile_src, tile_dst, leaf_rhs, leaf_inv, leaf_owner, anc_rhs, anc_inv, anc_owner):
    def leaf_solve(tree):
        blocks = []
        for block in range(WB):
            owner = leaf_owner[tree, block]
            blocks.append(jnp.dot(leaf_inv[tree, owner], leaf_rhs[tree, owner], preferred_element_type=jnp.float32).astype(jnp.bfloat16))
        return jnp.stack(blocks)

    leaf_x = lax.map(leaf_solve, jnp.arange(N_TREES, dtype=jnp.int32))
    solved = []
    for wave in range(1, WAVES):
        start = (wave - 1) * TW
        prior = jnp.stack(solved) if len(solved) > 0 else None

        def add_device(carry, index):
            tree = index // N_ROWS
            row = index % N_ROWS
            sources = leaf_x[tree]
            if prior is not None:
                sources = jnp.concatenate([sources, prior], 0)
            block_tiles = lax.dynamic_slice_in_dim(tiles[tree, row], start, TW, 0)
            src = lax.dynamic_slice_in_dim(tile_src[tree, row], start, TW, 0)
            dst = lax.dynamic_slice_in_dim(tile_dst[tree, row], start, TW, 0)
            picked = jnp.take(sources, src, axis=0)
            product = jnp.einsum("kij,kjr->kir", block_tiles.astype(jnp.float32), picked.astype(jnp.float32))
            onehot = (dst[:, None] == jnp.arange(WB, dtype=jnp.int32)[None, :]).astype(jnp.float32)
            return carry + jnp.einsum("kb,kir->bir", onehot, product), None

        update, unused = lax.scan(add_device, jnp.zeros((WB, B, R), jnp.float32), jnp.arange(N_TREES * N_ROWS, dtype=jnp.int32))
        for block in range(WB):
            owner = anc_owner[(wave - 1) * WB + block]
            shares = jnp.sum(anc_rhs[:, owner].astype(jnp.float32), axis=0)
            target = (shares - update[block]).astype(jnp.bfloat16)
            solved.append(jnp.dot(anc_inv[owner], target, preferred_element_type=jnp.float32).astype(jnp.bfloat16))
    return jnp.stack(solved)
```

```python
import functools

import jax
import jax.numpy as jnp
from jax import lax
from jax.experimental import pallas as pl
from jax.experimental.pallas import tpu as pltpu
from jax.sharding import PartitionSpec as P

WAVES = 3
WB = 2
TW = 2
MESH = pl.DeviceIdType.MESH
F32 = jnp.float32
BF16 = jnp.bfloat16


def broadcast(block, axis, source):
    block = jnp.where(lax.axis_index(axis) == source, block, jnp.zeros_like(block))
    return lax.psum(block, axis)


def general_body(tiles, tile_src, tile_dst, leaf_rhs, leaf_inv, leaf_owner, anc_rhs, anc_inv, anc_owner):
    row_count = lax.axis_size("rows")
    here = lax.axis_index("rows")
    share = leaf_rhs.shape[-1] // row_count
    own_leaf = jnp.dot(leaf_inv[0, 0], leaf_rhs[0, 0], preferred_element_type=F32).astype(BF16)
    known = []
    for block in range(WB):
        known.append(broadcast(own_leaf, "rows", leaf_owner[0, block]))
    outputs = []
    for wave in range(1, WAVES):
        start = (wave - 1) * TW
        sources = jnp.stack(known)
        block_tiles = tiles[0, 0, start : start + TW]
        picked = jnp.take(sources, tile_src[0, 0, start : start + TW], axis=0)
        product = jnp.einsum("kij,kjr->kir", block_tiles, picked, preferred_element_type=F32)
        onehot = (
            tile_dst[0, 0, start : start + TW][:, None] == jnp.arange(WB, dtype=jnp.int32)[None, :]
        ).astype(F32)
        owners = anc_owner[(wave - 1) * WB : wave * WB]
        mine = (owners == here).astype(F32)
        partial_value = mine[:, None, None] * anc_rhs[0, 0].astype(F32)[None] - jnp.einsum(
            "kb,kir->bir", onehot, product
        )
        summed = lax.psum(partial_value, ("rows", "trees"))
        chosen = jnp.einsum("b,bir->ir", mine, summed).astype(BF16)
        local_x = jnp.dot(anc_inv[0], chosen, preferred_element_type=F32).astype(BF16)
        for block in range(WB):
            result = broadcast(local_x, "rows", owners[block])
            known.append(result)
            outputs.append(lax.dynamic_slice_in_dim(result, here * share, share, 1))
    return jnp.stack(outputs)


NT = (((1,), (1,)), ((), ()))


def kernel(
    n, nt, tiles_h, src, dst, rhs_h, linv_h, lown, arhs_h, ainv_h, aown, out,
    tiles, rhs, linv, arhs, ainv, own, leaf_rs, leaf_ag, inv_rs, inv_ag, known, u_send, u_recv, xs,
    lsem, ssem, rsem,
):
    r = lax.axis_index("rows")
    t = lax.axis_index("trees")
    depth = rhs.shape[0]
    count = rhs.shape[1]
    ch = depth // n
    share = count // n
    every = n * nt

    def peer(k):
        flat = lax.rem(r * nt + t + k, every)
        return flat // nt, lax.rem(flat, nt)

    barrier = pltpu.get_barrier_semaphore()

    @pl.loop(1, every)
    def _(k):
        pr, pt = peer(k)
        pl.semaphore_signal(barrier, inc=1, device_id=(pr, pt), device_id_type=MESH)

    loads = []
    for i, (a, b) in enumerate(
        ((linv_h.at[0, 0], linv), (rhs_h.at[0, 0], rhs), (ainv_h.at[0], ainv), (arhs_h.at[0, 0], arhs), (tiles_h.at[0, 0], tiles))
    ):
        c = pltpu.make_async_copy(a, b, lsem.at[i])
        c.start()
        loads.append(c)
    loads[0].wait()
    loads[1].wait()
    own_leaf = jnp.dot(linv[...], rhs[...], preferred_element_type=F32).astype(BF16)
    own[...] = own_leaf.reshape(n, ch, count)
    loads[2].wait()
    pl.semaphore_wait(barrier, every - 1)

    def rows_send(phase, make):
        @pl.loop(1, n)
        def _(k):
            j = lax.rem(r + k, n)
            a, b = make(j)
            pltpu.make_async_remote_copy(
                src_ref=a, dst_ref=b, send_sem=ssem.at[phase], recv_sem=rsem.at[phase],
                device_id=(j, t), device_id_type=MESH,
            ).start()

    def all_send(phase, make):
        @pl.loop(1, every)
        def _(k):
            pr, pt = peer(k)
            a, b = make(pr, pt)
            pltpu.make_async_remote_copy(
                src_ref=a, dst_ref=b, send_sem=ssem.at[phase], recv_sem=rsem.at[phase],
                device_id=(pr, pt), device_id_type=MESH,
            ).start()

    def landed(phase, view):
        pltpu.make_async_copy(view, view, rsem.at[phase]).wait()

    def sent(phase, view):
        pltpu.make_async_copy(view, view, ssem.at[phase]).wait()

    most = pl.ds(0, n - 1)
    rows_send(0, lambda j: (own.at[j], leaf_rs.at[r]))
    leaf_rs[r] = own[r]
    rows_send(1, lambda j: (ainv.at[pl.ds(pl.multiple_of(j * ch, ch), ch)], inv_rs.at[r]))
    inv_rs[r] = ainv[pl.ds(pl.multiple_of(r * ch, ch), ch), :]

    landed(0, leaf_rs.at[most])
    for b in range(WB):
        leaf_ag[r, b] = leaf_rs[lown[0, b]]
    rows_send(2, lambda j: (leaf_ag.at[r], leaf_ag.at[r]))
    landed(1, inv_rs.at[most])
    for w in range(WAVES - 1):
        inv_ag[w, r] = inv_rs[aown[w * WB + t]]
    rows_send(3, lambda j: (inv_ag.at[0, r], inv_ag.at[0, r]))

    loads[3].wait()
    loads[4].wait()
    arhs_t = arhs[...].astype(F32).T
    landed(2, leaf_ag.at[most])
    for b in range(WB):
        known[b] = leaf_ag[:, b].reshape(depth, count).astype(F32).T.astype(BF16)

    for w in range(WAVES - 1):
        up = 4 + 3 * w
        products = []
        for k in range(w * TW, (w + 1) * TW):
            products.append(
                lax.dot_general(known[src[0, 0, k]], tiles[k], NT, preferred_element_type=F32)
            )
        for b in range(WB):
            part = jnp.where(aown[w * WB + b] == r, arhs_t, 0.0)
            for k in range(TW):
                part = part - jnp.where(dst[0, 0, w * TW + k] == b, products[k], 0.0)
            u_send[w, b] = part.reshape(n, share, depth).astype(BF16)
        all_send(up, lambda pr, pt: (u_send.at[w, pt, pr], u_recv.at[w, r * nt + t]))
        u_recv[w, r * nt + t] = u_send[w, t, r]
        if w + 1 < WAVES - 1:
            rows_send(up + 1, lambda j: (inv_ag.at[w + 1, r], inv_ag.at[w + 1, r]))
        landed(up, u_recv.at[w, pl.ds(0, every - 1)])
        y = jnp.sum(u_recv[w].astype(F32), axis=0).astype(BF16)
        landed(3 if w == 0 else 4 + 3 * (w - 1) + 1, inv_ag.at[w, most])
        inv = inv_ag[w].reshape(depth, depth)
        x = lax.dot_general(y, inv, NT, preferred_element_type=F32).astype(BF16)
        xs[w, t, r] = x
        if w + 1 < WAVES - 1:
            all_send(up + 2, lambda pr, pt: (xs.at[w, t, r], xs.at[w, t, r]))
            landed(up + 2, u_recv.at[w, pl.ds(0, every - 1)])
            for b in range(WB):
                known[(w + 1) * WB + b] = xs[w, b].reshape(count, depth)
        else:
            last = up + 1
            pltpu.make_async_remote_copy(
                src_ref=xs.at[w, t, r], dst_ref=xs.at[w, t, r], send_sem=ssem.at[last],
                recv_sem=rsem.at[last], device_id=(r, 1 - t), device_id_type=MESH,
            ).start()
            landed(last, xs.at[w, 0, 0])
    for w in range(WAVES - 1):
        for b in range(WB):
            out[w * WB + b] = xs[w, b, r]

    sent(0, own.at[most])
    sent(1, inv_rs.at[most])
    sent(2, leaf_ag.at[most])
    sent(3, inv_ag.at[0, most])
    for w in range(WAVES - 1):
        up = 4 + 3 * w
        sent(up, u_recv.at[w, pl.ds(0, every - 1)])
        if w + 1 < WAVES - 1:
            sent(up + 1, inv_ag.at[w + 1, most])
            sent(up + 2, u_recv.at[w, pl.ds(0, every - 1)])
        else:
            sent(up + 1, xs.at[w, 0, 0])


def fast_body(n, nt, tiles, tile_src, tile_dst, leaf_rhs, leaf_inv, leaf_owner, anc_rhs, anc_inv, anc_owner):
    depth, count = leaf_rhs.shape[-2:]
    kinds = tiles.shape[2]
    ch, share, every = depth // n, count // n, n * nt
    waves = WAVES - 1
    phases = 4 + 3 * waves
    any_spec = pl.BlockSpec(memory_space=pl.ANY)
    smem = pl.BlockSpec(memory_space=pltpu.SMEM)
    found = pl.pallas_call(
        functools.partial(kernel, n, nt),
        out_shape=jax.ShapeDtypeStruct((waves * WB, share, depth), BF16),
        in_specs=[any_spec, smem, smem, any_spec, any_spec, smem, any_spec, any_spec, smem],
        out_specs=pl.BlockSpec(memory_space=pltpu.VMEM),
        scratch_shapes=[
            pltpu.VMEM((kinds, depth, depth), BF16),
            pltpu.VMEM((depth, count), BF16),
            pltpu.VMEM((depth, depth), BF16),
            pltpu.VMEM((depth, count), BF16),
            pltpu.VMEM((depth, depth), BF16),
            pltpu.VMEM((n, ch, count), BF16),
            pltpu.VMEM((n, ch, count), BF16),
            pltpu.VMEM((n, WB, ch, count), BF16),
            pltpu.VMEM((n, ch, depth), BF16),
            pltpu.VMEM((waves, n, ch, depth), BF16),
            pltpu.VMEM((WB * waves, count, depth), BF16),
            pltpu.VMEM((waves, WB, n, share, depth), BF16),
            pltpu.VMEM((waves, every, share, depth), BF16),
            pltpu.VMEM((waves, WB, n, share, depth), BF16),
            pltpu.SemaphoreType.DMA((5,)),
            pltpu.SemaphoreType.DMA((phases,)),
            pltpu.SemaphoreType.DMA((phases,)),
        ],
        compiler_params=pltpu.CompilerParams(collective_id=0, has_side_effects=True),
    )(tiles, tile_src, tile_dst, leaf_rhs, leaf_inv, leaf_owner, anc_rhs, anc_inv, anc_owner)
    return jnp.swapaxes(found, 1, 2)


def solution(mesh):
    n, nt = mesh.shape["rows"], mesh.shape["trees"]
    placed = (
        P("trees", "rows", None, None, None),
        P("trees", "rows", None),
        P("trees", "rows", None),
        P("trees", "rows", None, None),
        P("trees", "rows", None, None),
        P("trees", None),
        P("trees", "rows", None, None),
        P("rows", None, None),
        P(),
    )

    def body(*args):
        depth, count = args[3].shape[-2:]
        if nt == WB and depth % (16 * n) == 0 and count % (8 * n) == 0:
            return fast_body(n, nt, *args)
        return general_body(*args)

    return jax.shard_map(
        body, mesh=mesh, in_specs=placed, out_specs=P(None, None, "rows"), check_vma=False
    )
```

```python
import functools

import jax
import jax.numpy as jnp
from jax import lax
from jax.experimental import pallas as pl
from jax.experimental.pallas import tpu as pltpu
from jax.sharding import PartitionSpec as P

WAVES = 3
WB = 2
TW = 2
MESH = pl.DeviceIdType.MESH
F32 = jnp.float32
BF16 = jnp.bfloat16


def broadcast(block, axis, source):
    block = jnp.where(lax.axis_index(axis) == source, block, jnp.zeros_like(block))
    return lax.psum(block, axis)


def general_body(tiles, tile_src, tile_dst, leaf_rhs, leaf_inv, leaf_owner, anc_rhs, anc_inv, anc_owner):
    row_count = lax.axis_size("rows")
    here = lax.axis_index("rows")
    share = leaf_rhs.shape[-1] // row_count
    own_leaf = jnp.dot(leaf_inv[0, 0], leaf_rhs[0, 0], preferred_element_type=F32).astype(BF16)
    known = []
    for block in range(WB):
        known.append(broadcast(own_leaf, "rows", leaf_owner[0, block]))
    outputs = []
    for wave in range(1, WAVES):
        start = (wave - 1) * TW
        sources = jnp.stack(known)
        block_tiles = tiles[0, 0, start : start + TW]
        picked = jnp.take(sources, tile_src[0, 0, start : start + TW], axis=0)
        product = jnp.einsum("kij,kjr->kir", block_tiles, picked, preferred_element_type=F32)
        onehot = (
            tile_dst[0, 0, start : start + TW][:, None] == jnp.arange(WB, dtype=jnp.int32)[None, :]
        ).astype(F32)
        owners = anc_owner[(wave - 1) * WB : wave * WB]
        mine = (owners == here).astype(F32)
        partial_value = mine[:, None, None] * anc_rhs[0, 0].astype(F32)[None] - jnp.einsum(
            "kb,kir->bir", onehot, product
        )
        summed = lax.psum(partial_value, ("rows", "trees"))
        chosen = jnp.einsum("b,bir->ir", mine, summed).astype(BF16)
        local_x = jnp.dot(anc_inv[0], chosen, preferred_element_type=F32).astype(BF16)
        for block in range(WB):
            result = broadcast(local_x, "rows", owners[block])
            known.append(result)
            outputs.append(lax.dynamic_slice_in_dim(result, here * share, share, 1))
    return jnp.stack(outputs)


NT = (((1,), (1,)), ((), ()))


def kernel(
    n, nt, tiles_h, src, dst, rhs_h, linv_h, lown, arhs_h, ainv_h, aown, out,
    tiles, rhs, linv, arhs, ainv, own, leaf_rs, leaf_ag, inv_rs, inv_ag, known, u_send, u_recv, xs,
    lsem, ssem, rsem,
):
    r = lax.axis_index("rows")
    t = lax.axis_index("trees")
    depth = rhs.shape[0]
    count = rhs.shape[1]
    ch = depth // n
    share = count // n
    every = n * nt

    def partner(m):
        if n & (n - 1):
            return lax.rem(r + m, n)
        j = r
        bit = 1
        while bit < n:
            if m & bit:
                j = j + bit * (1 - 2 * lax.rem(r // bit, 2))
            bit *= 2
        return j

    others = [partner(m) for m in range(n - 1, 0, -1)]
    everyone = [(j, q) for j in others for q in (t, 1 - t)] + [(r, 1 - t)]

    barrier = pltpu.get_barrier_semaphore()
    for where in everyone:
        pl.semaphore_signal(barrier, inc=1, device_id=where, device_id_type=MESH)

    loads = []
    for i, (a, b) in enumerate(
        ((linv_h.at[0, 0], linv), (rhs_h.at[0, 0], rhs), (ainv_h.at[0], ainv), (arhs_h.at[0, 0], arhs), (tiles_h.at[0, 0], tiles))
    ):
        c = pltpu.make_async_copy(a, b, lsem.at[i])
        c.start()
        loads.append(c)
    loads[0].wait()
    loads[1].wait()
    own_leaf = jnp.dot(linv[...], rhs[...], preferred_element_type=F32)
    own[...] = own_leaf.T.astype(BF16).reshape(n, share, depth)
    loads[2].wait()
    pl.semaphore_wait(barrier, every - 1)

    def rows_send(phase, make):
        for j in others:
            a, b = make(j)
            pltpu.make_async_remote_copy(
                src_ref=a, dst_ref=b, send_sem=ssem.at[phase], recv_sem=rsem.at[phase],
                device_id=(j, t), device_id_type=MESH,
            ).start()

    def all_send(phase, make):
        for pr, pt in everyone:
            a, b = make(pr, pt)
            pltpu.make_async_remote_copy(
                src_ref=a, dst_ref=b, send_sem=ssem.at[phase], recv_sem=rsem.at[phase],
                device_id=(pr, pt), device_id_type=MESH,
            ).start()

    def landed(phase, view):
        pltpu.make_async_copy(view, view, rsem.at[phase]).wait()

    def sent(phase, view):
        pltpu.make_async_copy(view, view, ssem.at[phase]).wait()

    most = pl.ds(0, n - 1)
    rows_send(0, lambda j: (own.at[j], leaf_rs.at[r]))
    leaf_rs[r] = own[r]
    rows_send(1, lambda j: (ainv.at[pl.ds(pl.multiple_of(j * ch, ch), ch)], inv_rs.at[r]))
    inv_rs[r] = ainv[pl.ds(pl.multiple_of(r * ch, ch), ch), :]

    landed(0, leaf_rs.at[most])
    for b in range(WB):
        leaf_ag[r, b] = leaf_rs[lown[0, b]]
    rows_send(2, lambda j: (leaf_ag.at[r], leaf_ag.at[r]))
    landed(1, inv_rs.at[most])
    for w in range(WAVES - 1):
        inv_ag[w, r] = inv_rs[aown[w * WB + t]]
    rows_send(3, lambda j: (inv_ag.at[0, r], inv_ag.at[0, r]))

    loads[3].wait()
    loads[4].wait()
    arhs_t = arhs[...].astype(F32).T
    landed(2, leaf_ag.at[most])
    for b in range(WB):
        known[b] = leaf_ag[:, b].reshape(count, depth)

    for w in range(WAVES - 1):
        up = 4 + 3 * w
        products = []
        for k in range(w * TW, (w + 1) * TW):
            products.append(
                lax.dot_general(known[src[0, 0, k]], tiles[k], NT, preferred_element_type=F32)
            )
        for b in range(WB):
            part = jnp.where(aown[w * WB + b] == r, arhs_t, 0.0)
            for k in range(TW):
                part = part - jnp.where(dst[0, 0, w * TW + k] == b, products[k], 0.0)
            u_send[w, b] = part.reshape(n, share, depth).astype(BF16)
        all_send(up, lambda pr, pt: (u_send.at[w, pt, pr], u_recv.at[w, r * nt + t]))
        u_recv[w, r * nt + t] = u_send[w, t, r]
        if w + 1 < WAVES - 1:
            rows_send(up + 1, lambda j: (inv_ag.at[w + 1, r], inv_ag.at[w + 1, r]))
        landed(up, u_recv.at[w, pl.ds(0, every - 1)])
        y = jnp.sum(u_recv[w].astype(F32), axis=0).astype(BF16)
        landed(3 if w == 0 else 4 + 3 * (w - 1) + 1, inv_ag.at[w, most])
        inv = inv_ag[w].reshape(depth, depth)
        x = lax.dot_general(y, inv, NT, preferred_element_type=F32).astype(BF16)
        xs[w, t, r] = x
        if w + 1 < WAVES - 1:
            all_send(up + 2, lambda pr, pt: (xs.at[w, t, r], xs.at[w, t, r]))
            landed(up + 2, u_recv.at[w, pl.ds(0, every - 1)])
            for b in range(WB):
                known[(w + 1) * WB + b] = xs[w, b].reshape(count, depth)
        else:
            last = up + 1
            pltpu.make_async_remote_copy(
                src_ref=xs.at[w, t, r], dst_ref=xs.at[w, t, r], send_sem=ssem.at[last],
                recv_sem=rsem.at[last], device_id=(r, 1 - t), device_id_type=MESH,
            ).start()
            landed(last, xs.at[w, 0, 0])
    for w in range(WAVES - 1):
        for b in range(WB):
            out[w * WB + b] = xs[w, b, r]

    sent(0, own.at[most])
    sent(1, inv_rs.at[most])
    sent(2, leaf_ag.at[most])
    sent(3, inv_ag.at[0, most])
    for w in range(WAVES - 1):
        up = 4 + 3 * w
        sent(up, u_recv.at[w, pl.ds(0, every - 1)])
        if w + 1 < WAVES - 1:
            sent(up + 1, inv_ag.at[w + 1, most])
            sent(up + 2, u_recv.at[w, pl.ds(0, every - 1)])
        else:
            sent(up + 1, xs.at[w, 0, 0])


def fast_body(n, nt, tiles, tile_src, tile_dst, leaf_rhs, leaf_inv, leaf_owner, anc_rhs, anc_inv, anc_owner):
    depth, count = leaf_rhs.shape[-2:]
    kinds = tiles.shape[2]
    ch, share, every = depth // n, count // n, n * nt
    waves = WAVES - 1
    phases = 4 + 3 * waves
    any_spec = pl.BlockSpec(memory_space=pl.ANY)
    smem = pl.BlockSpec(memory_space=pltpu.SMEM)
    found = pl.pallas_call(
        functools.partial(kernel, n, nt),
        out_shape=jax.ShapeDtypeStruct((waves * WB, share, depth), BF16),
        in_specs=[any_spec, smem, smem, any_spec, any_spec, smem, any_spec, any_spec, smem],
        out_specs=pl.BlockSpec(memory_space=pltpu.VMEM),
        scratch_shapes=[
            pltpu.VMEM((kinds, depth, depth), BF16),
            pltpu.VMEM((depth, count), BF16),
            pltpu.VMEM((depth, depth), BF16),
            pltpu.VMEM((depth, count), BF16),
            pltpu.VMEM((depth, depth), BF16),
            pltpu.VMEM((n, share, depth), BF16),
            pltpu.VMEM((n, share, depth), BF16),
            pltpu.VMEM((n, WB, share, depth), BF16),
            pltpu.VMEM((n, ch, depth), BF16),
            pltpu.VMEM((waves, n, ch, depth), BF16),
            pltpu.VMEM((WB * waves, count, depth), BF16),
            pltpu.VMEM((waves, WB, n, share, depth), BF16),
            pltpu.VMEM((waves, every, share, depth), BF16),
            pltpu.VMEM((waves, WB, n, share, depth), BF16),
            pltpu.SemaphoreType.DMA((5,)),
            pltpu.SemaphoreType.DMA((phases,)),
            pltpu.SemaphoreType.DMA((phases,)),
        ],
        compiler_params=pltpu.CompilerParams(collective_id=0, has_side_effects=True),
    )(tiles, tile_src, tile_dst, leaf_rhs, leaf_inv, leaf_owner, anc_rhs, anc_inv, anc_owner)
    return jnp.swapaxes(found, 1, 2)


def solution(mesh):
    n, nt = mesh.shape["rows"], mesh.shape["trees"]
    placed = (
        P("trees", "rows", None, None, None),
        P("trees", "rows", None),
        P("trees", "rows", None),
        P("trees", "rows", None, None),
        P("trees", "rows", None, None),
        P("trees", None),
        P("trees", "rows", None, None),
        P("rows", None, None),
        P(),
    )

    def body(*args):
        depth, count = args[3].shape[-2:]
        if nt == WB and depth % (16 * n) == 0 and count % (8 * n) == 0:
            return fast_body(n, nt, *args)
        return general_body(*args)

    return jax.shard_map(
        body, mesh=mesh, in_specs=placed, out_specs=P(None, None, "rows"), check_vma=False
    )
```

```python
import functools

import jax
import jax.numpy as jnp
from jax import lax
from jax.experimental import pallas as pl
from jax.experimental.pallas import tpu as pltpu
from jax.sharding import PartitionSpec as P

WAVES = 3
WB = 2
TW = 2
MESH = pl.DeviceIdType.MESH
F32 = jnp.float32
BF16 = jnp.bfloat16


def broadcast(block, axis, source):
    block = jnp.where(lax.axis_index(axis) == source, block, jnp.zeros_like(block))
    return lax.psum(block, axis)


def general_body(tiles, tile_src, tile_dst, leaf_rhs, leaf_inv, leaf_owner, anc_rhs, anc_inv, anc_owner):
    row_count = lax.axis_size("rows")
    here = lax.axis_index("rows")
    share = leaf_rhs.shape[-1] // row_count
    own_leaf = jnp.dot(leaf_inv[0, 0], leaf_rhs[0, 0], preferred_element_type=F32).astype(BF16)
    known = []
    for block in range(WB):
        known.append(broadcast(own_leaf, "rows", leaf_owner[0, block]))
    outputs = []
    for wave in range(1, WAVES):
        start = (wave - 1) * TW
        sources = jnp.stack(known)
        block_tiles = tiles[0, 0, start : start + TW]
        picked = jnp.take(sources, tile_src[0, 0, start : start + TW], axis=0)
        product = jnp.einsum("kij,kjr->kir", block_tiles, picked, preferred_element_type=F32)
        onehot = (
            tile_dst[0, 0, start : start + TW][:, None] == jnp.arange(WB, dtype=jnp.int32)[None, :]
        ).astype(F32)
        owners = anc_owner[(wave - 1) * WB : wave * WB]
        mine = (owners == here).astype(F32)
        partial_value = mine[:, None, None] * anc_rhs[0, 0].astype(F32)[None] - jnp.einsum(
            "kb,kir->bir", onehot, product
        )
        summed = lax.psum(partial_value, ("rows", "trees"))
        chosen = jnp.einsum("b,bir->ir", mine, summed).astype(BF16)
        local_x = jnp.dot(anc_inv[0], chosen, preferred_element_type=F32).astype(BF16)
        for block in range(WB):
            result = broadcast(local_x, "rows", owners[block])
            known.append(result)
            outputs.append(lax.dynamic_slice_in_dim(result, here * share, share, 1))
    return jnp.stack(outputs)


NT = (((1,), (1,)), ((), ()))


def kernel(
    n, nt, tiles_h, src, dst, rhs_h, linv_h, lown, arhs_h, ainv_h, aown, out,
    tiles, rhs, linv, arhs, ainv, own, leaf_rs, leaf_ag, inv_rs, inv_half, inv_ag, known, u_send, u_recv, xs,
    lsem, ssem, rsem,
):
    r = lax.axis_index("rows")
    t = lax.axis_index("trees")
    depth = rhs.shape[0]
    count = rhs.shape[1]
    ch = depth // n
    share = count // n
    every = n * nt

    def partner(m):
        if n & (n - 1):
            return lax.rem(r + m, n)
        j = r
        bit = 1
        while bit < n:
            if m & bit:
                j = j + bit * (1 - 2 * lax.rem(r // bit, 2))
            bit *= 2
        return j

    others = [partner(m) for m in range(n - 1, 0, -1)]
    everyone = [(j, q) for j in others for q in (t, 1 - t)] + [(r, 1 - t)]

    barrier = pltpu.get_barrier_semaphore()
    for where in everyone:
        pl.semaphore_signal(barrier, inc=1, device_id=where, device_id_type=MESH)

    loads = []
    for i, (a, b) in enumerate(
        ((linv_h.at[0, 0], linv), (rhs_h.at[0, 0], rhs), (ainv_h.at[0], ainv), (arhs_h.at[0, 0], arhs), (tiles_h.at[0, 0], tiles))
    ):
        c = pltpu.make_async_copy(a, b, lsem.at[i])
        c.start()
        loads.append(c)
    loads[0].wait()
    loads[1].wait()
    own_leaf = jnp.dot(linv[...], rhs[...], preferred_element_type=F32)
    own[...] = own_leaf.T.astype(BF16).reshape(n, share, depth)
    loads[2].wait()
    pl.semaphore_wait(barrier, every - 1)

    def rows_send(phase, make):
        for j in others:
            a, b = make(j)
            pltpu.make_async_remote_copy(
                src_ref=a, dst_ref=b, send_sem=ssem.at[phase], recv_sem=rsem.at[phase],
                device_id=(j, t), device_id_type=MESH,
            ).start()

    def all_send(phase, make):
        for pr, pt in everyone:
            a, b = make(pr, pt)
            pltpu.make_async_remote_copy(
                src_ref=a, dst_ref=b, send_sem=ssem.at[phase], recv_sem=rsem.at[phase],
                device_id=(pr, pt), device_id_type=MESH,
            ).start()

    def landed(phase, view):
        pltpu.make_async_copy(view, view, rsem.at[phase]).wait()

    def sent(phase, view):
        pltpu.make_async_copy(view, view, ssem.at[phase]).wait()

    most = pl.ds(0, n - 1)
    inner = 1
    while inner * inner * 4 <= n and n % (inner * 2) == 0:
        inner *= 2
    outer = n // inner
    ro, ri = r // inner, lax.rem(r, inner)
    chunk = ri * outer + ro
    lanes_each = depth // nt
    lanes = pl.ds(pl.multiple_of(t * lanes_each, lanes_each), lanes_each)

    def inv_part(j):
        at = (lax.rem(j, inner) * outer + j // inner) * ch
        return pl.ds(pl.multiple_of(at, ch), ch)

    def push(phase, a, b, where):
        pltpu.make_async_remote_copy(
            src_ref=a, dst_ref=b, send_sem=ssem.at[phase], recv_sem=rsem.at[phase],
            device_id=where, device_id_type=MESH,
        ).start()

    def inner_send(w, phase):
        held = pl.ds(ri * outer, outer)
        for k in range(1, inner):
            to = ro * inner + lax.rem(ri + k, inner)
            push(phase, inv_ag.at[w, held], inv_ag.at[w, held], (to, t))

    inner_view = inv_ag.at[0, pl.ds(0, (inner - 1) * outer)]
    outer_view = inv_ag.at[0, pl.ds(0, (outer - 1) * (WAVES - 1))]
    last = 4 + 3 * (WAVES - 1)
    swap = last + 1
    rows_send(0, lambda j: (own.at[j], leaf_rs.at[r]))
    leaf_rs[r] = own[r]
    rows_send(1, lambda j: (ainv.at[inv_part(j), lanes], inv_rs.at[r]))
    inv_rs[r] = ainv[inv_part(r), lanes]

    landed(0, leaf_rs.at[most])
    for b in range(WB):
        leaf_ag[r, b] = leaf_rs[lown[0, b]]
    rows_send(2, lambda j: (leaf_ag.at[r], leaf_ag.at[r]))
    landed(1, inv_rs.at[most])
    for w in range(WAVES - 1):
        inv_half[w] = inv_rs[aown[w * WB + 1 - t]]
        push(swap, inv_half.at[w], inv_ag.at[w, chunk, :, lanes], (r, 1 - t))
    for w in range(WAVES - 1):
        inv_ag[w, chunk, :, lanes] = inv_rs[aown[w * WB + t]]
    landed(swap, inv_half)
    for k in range(1, outer):
        to = lax.rem(ro + k, outer) * inner + ri
        for w in range(WAVES - 1):
            push(3, inv_ag.at[w, chunk], inv_ag.at[w, chunk], (to, t))

    loads[3].wait()
    loads[4].wait()
    arhs_t = arhs[...].astype(F32).T
    landed(2, leaf_ag.at[most])
    for b in range(WB):
        known[b] = leaf_ag[:, b].reshape(count, depth)

    for w in range(WAVES - 1):
        up = 4 + 3 * w
        products = []
        for k in range(w * TW, (w + 1) * TW):
            products.append(
                lax.dot_general(known[src[0, 0, k]], tiles[k], NT, preferred_element_type=F32)
            )
        for b in range(WB):
            part = jnp.where(aown[w * WB + b] == r, arhs_t, 0.0)
            for k in range(TW):
                part = part - jnp.where(dst[0, 0, w * TW + k] == b, products[k], 0.0)
            u_send[w, b] = part.reshape(n, share, depth).astype(BF16)
        all_send(up, lambda pr, pt: (u_send.at[w, pt, pr], u_recv.at[w, r * nt + t]))
        u_recv[w, r * nt + t] = u_send[w, t, r]
        if w == 0:
            landed(3, outer_view)
            inner_send(0, up + 1)
        landed(up, u_recv.at[w, pl.ds(0, every - 1)])
        y = jnp.sum(u_recv[w].astype(F32), axis=0).astype(BF16)
        landed(up + 1, inner_view)
        inv = inv_ag[w].reshape(depth, depth)
        x = lax.dot_general(y, inv, NT, preferred_element_type=F32).astype(BF16)
        xs[w, t, r] = x
        if w + 1 < WAVES - 1:
            all_send(up + 2, lambda pr, pt: (xs.at[w, t, r], xs.at[w, t, r]))
            inner_send(w + 1, up + 4)
            landed(up + 2, u_recv.at[w, pl.ds(0, every - 1)])
            for b in range(WB):
                known[(w + 1) * WB + b] = xs[w, b].reshape(count, depth)
        else:
            pltpu.make_async_remote_copy(
                src_ref=xs.at[w, t, r], dst_ref=xs.at[w, t, r], send_sem=ssem.at[last],
                recv_sem=rsem.at[last], device_id=(r, 1 - t), device_id_type=MESH,
            ).start()
            landed(last, xs.at[w, 0, 0])
    for w in range(WAVES - 1):
        for b in range(WB):
            out[w * WB + b] = xs[w, b, r]

    sent(0, own.at[most])
    sent(1, inv_rs.at[most])
    sent(2, leaf_ag.at[most])
    sent(3, outer_view)
    sent(swap, inv_half)
    sent(last, xs.at[0, 0, 0])
    for w in range(WAVES - 1):
        up = 4 + 3 * w
        sent(up, u_recv.at[w, pl.ds(0, every - 1)])
        sent(up + 1, inner_view)
        if w + 1 < WAVES - 1:
            sent(up + 2, u_recv.at[w, pl.ds(0, every - 1)])


def fast_body(n, nt, tiles, tile_src, tile_dst, leaf_rhs, leaf_inv, leaf_owner, anc_rhs, anc_inv, anc_owner):
    depth, count = leaf_rhs.shape[-2:]
    kinds = tiles.shape[2]
    ch, share, every = depth // n, count // n, n * nt
    waves = WAVES - 1
    phases = 6 + 3 * waves
    any_spec = pl.BlockSpec(memory_space=pl.ANY)
    smem = pl.BlockSpec(memory_space=pltpu.SMEM)
    found = pl.pallas_call(
        functools.partial(kernel, n, nt),
        out_shape=jax.ShapeDtypeStruct((waves * WB, share, depth), BF16),
        in_specs=[any_spec, smem, smem, any_spec, any_spec, smem, any_spec, any_spec, smem],
        out_specs=pl.BlockSpec(memory_space=pltpu.VMEM),
        scratch_shapes=[
            pltpu.VMEM((kinds, depth, depth), BF16),
            pltpu.VMEM((depth, count), BF16),
            pltpu.VMEM((depth, depth), BF16),
            pltpu.VMEM((depth, count), BF16),
            pltpu.VMEM((depth, depth), BF16),
            pltpu.VMEM((n, share, depth), BF16),
            pltpu.VMEM((n, share, depth), BF16),
            pltpu.VMEM((n, WB, share, depth), BF16),
            pltpu.VMEM((n, ch, depth // nt), BF16),
            pltpu.VMEM((waves, ch, depth // nt), BF16),
            pltpu.VMEM((waves, n, ch, depth), BF16),
            pltpu.VMEM((WB * waves, count, depth), BF16),
            pltpu.VMEM((waves, WB, n, share, depth), BF16),
            pltpu.VMEM((waves, every, share, depth), BF16),
            pltpu.VMEM((waves, WB, n, share, depth), BF16),
            pltpu.SemaphoreType.DMA((5,)),
            pltpu.SemaphoreType.DMA((phases,)),
            pltpu.SemaphoreType.DMA((phases,)),
        ],
        compiler_params=pltpu.CompilerParams(collective_id=0, has_side_effects=True),
    )(tiles, tile_src, tile_dst, leaf_rhs, leaf_inv, leaf_owner, anc_rhs, anc_inv, anc_owner)
    return jnp.swapaxes(found, 1, 2)


def solution(mesh):
    n, nt = mesh.shape["rows"], mesh.shape["trees"]
    placed = (
        P("trees", "rows", None, None, None),
        P("trees", "rows", None),
        P("trees", "rows", None),
        P("trees", "rows", None, None),
        P("trees", "rows", None, None),
        P("trees", None),
        P("trees", "rows", None, None),
        P("rows", None, None),
        P(),
    )

    def body(*args):
        depth, count = args[3].shape[-2:]
        if nt == WB and n > 3 and depth % (16 * n) == 0 and depth % (128 * nt) == 0 and count % (8 * n) == 0:
            return fast_body(n, nt, *args)
        return general_body(*args)

    return jax.shard_map(
        body, mesh=mesh, in_specs=placed, out_specs=P(None, None, "rows"), check_vma=False
    )
```

```python
import functools

import jax
import jax.numpy as jnp
from jax import lax
from jax.experimental import pallas as pl
from jax.experimental.pallas import tpu as pltpu
from jax.sharding import PartitionSpec as P

WAVES = 3
WB = 2
TW = 2
MESH = pl.DeviceIdType.MESH
F32 = jnp.float32
BF16 = jnp.bfloat16


def broadcast(block, axis, source):
    block = jnp.where(lax.axis_index(axis) == source, block, jnp.zeros_like(block))
    return lax.psum(block, axis)


def general_body(tiles, tile_src, tile_dst, leaf_rhs, leaf_inv, leaf_owner, anc_rhs, anc_inv, anc_owner):
    row_count = lax.axis_size("rows")
    here = lax.axis_index("rows")
    share = leaf_rhs.shape[-1] // row_count
    own_leaf = jnp.dot(leaf_inv[0, 0], leaf_rhs[0, 0], preferred_element_type=F32).astype(BF16)
    known = []
    for block in range(WB):
        known.append(broadcast(own_leaf, "rows", leaf_owner[0, block]))
    outputs = []
    for wave in range(1, WAVES):
        start = (wave - 1) * TW
        sources = jnp.stack(known)
        block_tiles = tiles[0, 0, start : start + TW]
        picked = jnp.take(sources, tile_src[0, 0, start : start + TW], axis=0)
        product = jnp.einsum("kij,kjr->kir", block_tiles, picked, preferred_element_type=F32)
        onehot = (
            tile_dst[0, 0, start : start + TW][:, None] == jnp.arange(WB, dtype=jnp.int32)[None, :]
        ).astype(F32)
        owners = anc_owner[(wave - 1) * WB : wave * WB]
        mine = (owners == here).astype(F32)
        partial_value = mine[:, None, None] * anc_rhs[0, 0].astype(F32)[None] - jnp.einsum(
            "kb,kir->bir", onehot, product
        )
        summed = lax.psum(partial_value, ("rows", "trees"))
        chosen = jnp.einsum("b,bir->ir", mine, summed).astype(BF16)
        local_x = jnp.dot(anc_inv[0], chosen, preferred_element_type=F32).astype(BF16)
        for block in range(WB):
            result = broadcast(local_x, "rows", owners[block])
            known.append(result)
            outputs.append(lax.dynamic_slice_in_dim(result, here * share, share, 1))
    return jnp.stack(outputs)


NT = (((1,), (1,)), ((), ()))


def kernel(
    n, nt, tiles_h, src, dst, rhs_h, linv_h, lown, arhs_h, ainv_h, aown, out,
    tiles, rhs, linv, arhs, ainv, own, leaf_rs, leaf_ag, inv_rs, inv_half, inv_ag, known, u_send, u_recv, xs,
    lsem, ssem, rsem,
):
    r = lax.axis_index("rows")
    t = lax.axis_index("trees")
    depth = rhs.shape[0]
    count = rhs.shape[1]
    ch = depth // n
    share = count // n
    every = n * nt

    def partner(m):
        if n & (n - 1):
            return lax.rem(r + m, n)
        j = r
        bit = 1
        while bit < n:
            if m & bit:
                j = j + bit * (1 - 2 * lax.rem(r // bit, 2))
            bit *= 2
        return j

    inner = 1
    while inner * inner * 4 <= n and n % (inner * 2) == 0:
        inner *= 2
    masks = sorted(range(1, n), key=lambda m: (-(m // inner + m % inner), m // inner))
    others = [partner(m) for m in masks]
    everyone = [(j, q) for j in others for q in (t, 1 - t)] + [(r, 1 - t)]

    barrier = pltpu.get_barrier_semaphore()
    for where in everyone:
        pl.semaphore_signal(barrier, inc=1, device_id=where, device_id_type=MESH)

    loads = []
    for i, (a, b) in enumerate(
        ((linv_h.at[0, 0], linv), (rhs_h.at[0, 0], rhs), (ainv_h.at[0], ainv), (arhs_h.at[0, 0], arhs), (tiles_h.at[0, 0], tiles))
    ):
        c = pltpu.make_async_copy(a, b, lsem.at[i])
        c.start()
        loads.append(c)
    loads[0].wait()
    loads[1].wait()
    own_leaf = jnp.dot(linv[...], rhs[...], preferred_element_type=F32)
    own[...] = own_leaf.T.astype(BF16).reshape(n, share, depth)
    loads[2].wait()
    pl.semaphore_wait(barrier, every - 1)

    def rows_send(phase, make):
        for j in others:
            a, b = make(j)
            pltpu.make_async_remote_copy(
                src_ref=a, dst_ref=b, send_sem=ssem.at[phase], recv_sem=rsem.at[phase],
                device_id=(j, t), device_id_type=MESH,
            ).start()

    def all_send(phase, make):
        for pr, pt in everyone:
            a, b = make(pr, pt)
            pltpu.make_async_remote_copy(
                src_ref=a, dst_ref=b, send_sem=ssem.at[phase], recv_sem=rsem.at[phase],
                device_id=(pr, pt), device_id_type=MESH,
            ).start()

    def landed(phase, view):
        pltpu.make_async_copy(view, view, rsem.at[phase]).wait()

    def sent(phase, view):
        pltpu.make_async_copy(view, view, ssem.at[phase]).wait()

    most = pl.ds(0, n - 1)
    outer = n // inner
    ro, ri = r // inner, lax.rem(r, inner)
    chunk = ri * outer + ro
    lanes_each = depth // nt
    lanes = pl.ds(pl.multiple_of(t * lanes_each, lanes_each), lanes_each)

    def inv_part(j):
        at = (lax.rem(j, inner) * outer + j // inner) * ch
        return pl.ds(pl.multiple_of(at, ch), ch)

    def push(phase, a, b, where):
        pltpu.make_async_remote_copy(
            src_ref=a, dst_ref=b, send_sem=ssem.at[phase], recv_sem=rsem.at[phase],
            device_id=where, device_id_type=MESH,
        ).start()

    def inner_send(w, phase):
        held = pl.ds(ri * outer, outer)
        for k in range(1, inner):
            to = ro * inner + lax.rem(ri + k, inner)
            push(phase, inv_ag.at[w, held], inv_ag.at[w, held], (to, t))

    inner_view = inv_ag.at[0, pl.ds(0, (inner - 1) * outer)]
    outer_view = inv_ag.at[0, pl.ds(0, (outer - 1) * (WAVES - 1))]
    last = 4 + 3 * (WAVES - 1)
    swap = last + 1
    rows_send(0, lambda j: (own.at[j], leaf_rs.at[r]))
    leaf_rs[r] = own[r]
    rows_send(1, lambda j: (ainv.at[inv_part(j), lanes], inv_rs.at[r]))
    inv_rs[r] = ainv[inv_part(r), lanes]

    landed(0, leaf_rs.at[most])
    for b in range(WB):
        leaf_ag[r, b] = leaf_rs[lown[0, b]]
    rows_send(2, lambda j: (leaf_ag.at[r], leaf_ag.at[r]))
    landed(1, inv_rs.at[most])
    for w in range(WAVES - 1):
        inv_half[w] = inv_rs[aown[w * WB + 1 - t]]
        push(swap, inv_half.at[w], inv_ag.at[w, chunk, :, lanes], (r, 1 - t))
    for w in range(WAVES - 1):
        inv_ag[w, chunk, :, lanes] = inv_rs[aown[w * WB + t]]
    landed(swap, inv_half)
    for k in range(1, outer):
        to = lax.rem(ro + k, outer) * inner + ri
        for w in range(WAVES - 1):
            push(3, inv_ag.at[w, chunk], inv_ag.at[w, chunk], (to, t))

    loads[3].wait()
    loads[4].wait()
    arhs_t = arhs[...].astype(F32).T
    landed(2, leaf_ag.at[most])
    for b in range(WB):
        known[b] = leaf_ag[:, b].reshape(count, depth)

    for w in range(WAVES - 1):
        up = 4 + 3 * w
        products = []
        for k in range(w * TW, (w + 1) * TW):
            products.append(
                lax.dot_general(known[src[0, 0, k]], tiles[k], NT, preferred_element_type=F32)
            )
        for b in range(WB):
            part = jnp.where(aown[w * WB + b] == r, arhs_t, 0.0)
            for k in range(TW):
                part = part - jnp.where(dst[0, 0, w * TW + k] == b, products[k], 0.0)
            u_send[w, b] = part.reshape(n, share, depth).astype(BF16)
        all_send(up, lambda pr, pt: (u_send.at[w, pt, pr], u_recv.at[w, r * nt + t]))
        u_recv[w, r * nt + t] = u_send[w, t, r]
        if w == 0:
            landed(3, outer_view)
            inner_send(0, up + 1)
        landed(up, u_recv.at[w, pl.ds(0, every - 1)])
        y = jnp.sum(u_recv[w].astype(F32), axis=0).astype(BF16)
        landed(up + 1, inner_view)
        inv = inv_ag[w].reshape(depth, depth)
        x = lax.dot_general(y, inv, NT, preferred_element_type=F32).astype(BF16)
        xs[w, t, r] = x
        if w + 1 < WAVES - 1:
            all_send(up + 2, lambda pr, pt: (xs.at[w, t, r], xs.at[w, t, r]))
            inner_send(w + 1, up + 4)
            landed(up + 2, u_recv.at[w, pl.ds(0, every - 1)])
            for b in range(WB):
                known[(w + 1) * WB + b] = xs[w, b].reshape(count, depth)
        else:
            pltpu.make_async_remote_copy(
                src_ref=xs.at[w, t, r], dst_ref=xs.at[w, t, r], send_sem=ssem.at[last],
                recv_sem=rsem.at[last], device_id=(r, 1 - t), device_id_type=MESH,
            ).start()
            landed(last, xs.at[w, 0, 0])
    for w in range(WAVES - 1):
        for b in range(WB):
            out[w * WB + b] = xs[w, b, r]

    sent(0, own.at[most])
    sent(1, inv_rs.at[most])
    sent(2, leaf_ag.at[most])
    sent(3, outer_view)
    sent(swap, inv_half)
    sent(last, xs.at[0, 0, 0])
    for w in range(WAVES - 1):
        up = 4 + 3 * w
        sent(up, u_recv.at[w, pl.ds(0, every - 1)])
        sent(up + 1, inner_view)
        if w + 1 < WAVES - 1:
            sent(up + 2, u_recv.at[w, pl.ds(0, every - 1)])


def fast_body(n, nt, tiles, tile_src, tile_dst, leaf_rhs, leaf_inv, leaf_owner, anc_rhs, anc_inv, anc_owner):
    depth, count = leaf_rhs.shape[-2:]
    kinds = tiles.shape[2]
    ch, share, every = depth // n, count // n, n * nt
    waves = WAVES - 1
    phases = 6 + 3 * waves
    any_spec = pl.BlockSpec(memory_space=pl.ANY)
    smem = pl.BlockSpec(memory_space=pltpu.SMEM)
    found = pl.pallas_call(
        functools.partial(kernel, n, nt),
        out_shape=jax.ShapeDtypeStruct((waves * WB, share, depth), BF16),
        in_specs=[any_spec, smem, smem, any_spec, any_spec, smem, any_spec, any_spec, smem],
        out_specs=pl.BlockSpec(memory_space=pltpu.VMEM),
        scratch_shapes=[
            pltpu.VMEM((kinds, depth, depth), BF16),
            pltpu.VMEM((depth, count), BF16),
            pltpu.VMEM((depth, depth), BF16),
            pltpu.VMEM((depth, count), BF16),
            pltpu.VMEM((depth, depth), BF16),
            pltpu.VMEM((n, share, depth), BF16),
            pltpu.VMEM((n, share, depth), BF16),
            pltpu.VMEM((n, WB, share, depth), BF16),
            pltpu.VMEM((n, ch, depth // nt), BF16),
            pltpu.VMEM((waves, ch, depth // nt), BF16),
            pltpu.VMEM((waves, n, ch, depth), BF16),
            pltpu.VMEM((WB * waves, count, depth), BF16),
            pltpu.VMEM((waves, WB, n, share, depth), BF16),
            pltpu.VMEM((waves, every, share, depth), BF16),
            pltpu.VMEM((waves, WB, n, share, depth), BF16),
            pltpu.SemaphoreType.DMA((5,)),
            pltpu.SemaphoreType.DMA((phases,)),
            pltpu.SemaphoreType.DMA((phases,)),
        ],
        compiler_params=pltpu.CompilerParams(collective_id=0, has_side_effects=True),
    )(tiles, tile_src, tile_dst, leaf_rhs, leaf_inv, leaf_owner, anc_rhs, anc_inv, anc_owner)
    return jnp.swapaxes(found, 1, 2)


def solution(mesh):
    n, nt = mesh.shape["rows"], mesh.shape["trees"]
    placed = (
        P("trees", "rows", None, None, None),
        P("trees", "rows", None),
        P("trees", "rows", None),
        P("trees", "rows", None, None),
        P("trees", "rows", None, None),
        P("trees", None),
        P("trees", "rows", None, None),
        P("rows", None, None),
        P(),
    )

    def body(*args):
        depth, count = args[3].shape[-2:]
        if nt == WB and n > 3 and depth % (16 * n) == 0 and depth % (128 * nt) == 0 and count % (8 * n) == 0:
            return fast_body(n, nt, *args)
        return general_body(*args)

    return jax.shard_map(
        body, mesh=mesh, in_specs=placed, out_specs=P(None, None, "rows"), check_vma=False
    )
```

```python
import functools

import jax
import jax.numpy as jnp
from jax import lax
from jax.experimental import pallas as pl
from jax.experimental.pallas import tpu as pltpu
from jax.sharding import PartitionSpec as P

WAVES = 3
WB = 2
TW = 2
MESH = pl.DeviceIdType.MESH
F32 = jnp.float32
BF16 = jnp.bfloat16


def broadcast(block, axis, source):
    block = jnp.where(lax.axis_index(axis) == source, block, jnp.zeros_like(block))
    return lax.psum(block, axis)


def general_body(tiles, tile_src, tile_dst, leaf_rhs, leaf_inv, leaf_owner, anc_rhs, anc_inv, anc_owner):
    row_count = lax.axis_size("rows")
    here = lax.axis_index("rows")
    share = leaf_rhs.shape[-1] // row_count
    own_leaf = jnp.dot(leaf_inv[0, 0], leaf_rhs[0, 0], preferred_element_type=F32).astype(BF16)
    known = []
    for block in range(WB):
        known.append(broadcast(own_leaf, "rows", leaf_owner[0, block]))
    outputs = []
    for wave in range(1, WAVES):
        start = (wave - 1) * TW
        sources = jnp.stack(known)
        block_tiles = tiles[0, 0, start : start + TW]
        picked = jnp.take(sources, tile_src[0, 0, start : start + TW], axis=0)
        product = jnp.einsum("kij,kjr->kir", block_tiles, picked, preferred_element_type=F32)
        onehot = (
            tile_dst[0, 0, start : start + TW][:, None] == jnp.arange(WB, dtype=jnp.int32)[None, :]
        ).astype(F32)
        owners = anc_owner[(wave - 1) * WB : wave * WB]
        mine = (owners == here).astype(F32)
        partial_value = mine[:, None, None] * anc_rhs[0, 0].astype(F32)[None] - jnp.einsum(
            "kb,kir->bir", onehot, product
        )
        summed = lax.psum(partial_value, ("rows", "trees"))
        chosen = jnp.einsum("b,bir->ir", mine, summed).astype(BF16)
        local_x = jnp.dot(anc_inv[0], chosen, preferred_element_type=F32).astype(BF16)
        for block in range(WB):
            result = broadcast(local_x, "rows", owners[block])
            known.append(result)
            outputs.append(lax.dynamic_slice_in_dim(result, here * share, share, 1))
    return jnp.stack(outputs)


NT = (((1,), (1,)), ((), ()))


def kernel(
    n, nt, tiles_h, src, dst, rhs_h, linv_h, lown, arhs_h, ainv_h, aown, out,
    tiles, rhs, linv, arhs, ainv, own, leaf_rs, leaf_ag, inv_rs, inv_half, inv_ag, known, u_send, u_recv, xs,
    lsem, ssem, rsem,
):
    r = lax.axis_index("rows")
    t = lax.axis_index("trees")
    depth = rhs.shape[0]
    count = rhs.shape[1]
    ch = depth // n
    share = count // n
    every = n * nt

    def partner(m):
        if n & (n - 1):
            return lax.rem(r + m, n)
        j = r
        bit = 1
        while bit < n:
            if m & bit:
                j = j + bit * (1 - 2 * lax.rem(r // bit, 2))
            bit *= 2
        return j

    inner = 1
    while inner * inner * 4 <= n and n % (inner * 2) == 0:
        inner *= 2
    masks = sorted(range(1, n), key=lambda m: (-(m // inner + m % inner), m // inner))
    others = [partner(m) for m in masks]
    everyone = [(j, q) for j in others for q in (t, 1 - t)] + [(r, 1 - t)]

    barrier = pltpu.get_barrier_semaphore()
    for where in everyone:
        pl.semaphore_signal(barrier, inc=1, device_id=where, device_id_type=MESH)

    loads = []
    for i, (a, b) in enumerate(
        ((linv_h.at[0, 0], linv), (rhs_h.at[0, 0], rhs), (ainv_h.at[0], ainv), (arhs_h.at[0, 0], arhs), (tiles_h.at[0, 0], tiles))
    ):
        c = pltpu.make_async_copy(a, b, lsem.at[i])
        c.start()
        loads.append(c)
    loads[0].wait()
    loads[1].wait()
    own_leaf = jnp.dot(linv[...], rhs[...], preferred_element_type=F32)
    own[...] = own_leaf.T.astype(BF16).reshape(n, share, depth)
    loads[2].wait()
    pl.semaphore_wait(barrier, every - 1)

    def rows_send(phase, make):
        for j in others:
            a, b = make(j)
            pltpu.make_async_remote_copy(
                src_ref=a, dst_ref=b, send_sem=ssem.at[phase], recv_sem=rsem.at[phase],
                device_id=(j, t), device_id_type=MESH,
            ).start()

    def all_send(phase, make):
        for pr, pt in everyone:
            a, b = make(pr, pt)
            pltpu.make_async_remote_copy(
                src_ref=a, dst_ref=b, send_sem=ssem.at[phase], recv_sem=rsem.at[phase],
                device_id=(pr, pt), device_id_type=MESH,
            ).start()

    def landed(phase, view):
        pltpu.make_async_copy(view, view, rsem.at[phase]).wait()

    def sent(phase, view):
        pltpu.make_async_copy(view, view, ssem.at[phase]).wait()

    most = pl.ds(0, n - 1)
    outer = n // inner
    ro, ri = r // inner, lax.rem(r, inner)
    chunk = ri * outer + ro
    lanes_each = depth // nt
    lanes = pl.ds(pl.multiple_of(t * lanes_each, lanes_each), lanes_each)

    def inv_part(j):
        at = (lax.rem(j, inner) * outer + j // inner) * ch
        return pl.ds(pl.multiple_of(at, ch), ch)

    def push(phase, a, b, where):
        pltpu.make_async_remote_copy(
            src_ref=a, dst_ref=b, send_sem=ssem.at[phase], recv_sem=rsem.at[phase],
            device_id=where, device_id_type=MESH,
        ).start()

    def inner_send(w, phase):
        held = pl.ds(ri * outer, outer)
        for k in range(1, inner):
            to = ro * inner + lax.rem(ri + k, inner)
            push(phase, inv_ag.at[w, held], inv_ag.at[w, held], (to, t))

    inner_view = inv_ag.at[0, pl.ds(0, (inner - 1) * outer)]
    outer_view = inv_ag.at[0, pl.ds(0, (outer - 1) * (WAVES - 1))]
    last = 4 + 3 * (WAVES - 1)
    swap = last + 1
    rows_send(0, lambda j: (own.at[j], leaf_rs.at[r]))
    leaf_rs[r] = own[r]
    rows_send(1, lambda j: (ainv.at[inv_part(j), lanes], inv_rs.at[r]))
    inv_rs[r] = ainv[inv_part(r), lanes]

    landed(0, leaf_rs.at[most])
    for b in range(WB):
        leaf_ag[r, b] = leaf_rs[lown[0, b]]
    rows_send(2, lambda j: (leaf_ag.at[r], leaf_ag.at[r]))
    landed(1, inv_rs.at[most])
    for w in range(WAVES - 1):
        inv_half[w] = inv_rs[aown[w * WB + 1 - t]]
        push(swap, inv_half.at[w], inv_ag.at[w, chunk, :, lanes], (r, 1 - t))
    for w in range(WAVES - 1):
        inv_ag[w, chunk, :, lanes] = inv_rs[aown[w * WB + t]]
    landed(swap, inv_half)
    for k in range(1, outer):
        to = lax.rem(ro + k, outer) * inner + ri
        for w in range(WAVES - 1):
            push(3, inv_ag.at[w, chunk], inv_ag.at[w, chunk], (to, t))

    loads[3].wait()
    loads[4].wait()
    arhs_t = arhs[...].astype(F32).T
    landed(2, leaf_ag.at[most])
    for b in range(WB):
        known[b] = leaf_ag[:, b].reshape(count, depth)

    for w in range(WAVES - 1):
        up = 4 + 3 * w
        products = []
        for k in range(w * TW, (w + 1) * TW):
            products.append(
                lax.dot_general(known[src[0, 0, k]], tiles[k], NT, preferred_element_type=F32)
            )
        for b in range(WB):
            part = jnp.where(aown[w * WB + b] == r, arhs_t, 0.0)
            for k in range(TW):
                part = part - jnp.where(dst[0, 0, w * TW + k] == b, products[k], 0.0)
            u_send[w, b] = part.reshape(n, share, depth).astype(BF16)
            for j in others:
                push(up, u_send.at[w, b, j], u_recv.at[w, r * nt + t], (j, b))
        push(up, u_send.at[w, 1 - t, r], u_recv.at[w, r * nt + t], (r, 1 - t))
        u_recv[w, r * nt + t] = u_send[w, t, r]
        if w == 0:
            landed(3, outer_view)
            inner_send(0, up + 1)
        landed(up, u_recv.at[w, pl.ds(0, every - 1)])
        y = jnp.sum(u_recv[w].astype(F32), axis=0).astype(BF16)
        landed(up + 1, inner_view)
        inv = inv_ag[w].reshape(depth, depth)
        x = lax.dot_general(y, inv, NT, preferred_element_type=F32).astype(BF16)
        xs[w, t, r] = x
        if w + 1 < WAVES - 1:
            all_send(up + 2, lambda pr, pt: (xs.at[w, t, r], xs.at[w, t, r]))
            inner_send(w + 1, up + 4)
            landed(up + 2, u_recv.at[w, pl.ds(0, every - 1)])
            for b in range(WB):
                known[(w + 1) * WB + b] = xs[w, b].reshape(count, depth)
        else:
            pltpu.make_async_remote_copy(
                src_ref=xs.at[w, t, r], dst_ref=xs.at[w, t, r], send_sem=ssem.at[last],
                recv_sem=rsem.at[last], device_id=(r, 1 - t), device_id_type=MESH,
            ).start()
            landed(last, xs.at[w, 0, 0])
    for w in range(WAVES - 1):
        for b in range(WB):
            out[w * WB + b] = xs[w, b, r]

    sent(0, own.at[most])
    sent(1, inv_rs.at[most])
    sent(2, leaf_ag.at[most])
    sent(3, outer_view)
    sent(swap, inv_half)
    sent(last, xs.at[0, 0, 0])
    for w in range(WAVES - 1):
        up = 4 + 3 * w
        sent(up, u_recv.at[w, pl.ds(0, every - 1)])
        sent(up + 1, inner_view)
        if w + 1 < WAVES - 1:
            sent(up + 2, u_recv.at[w, pl.ds(0, every - 1)])


def fast_body(n, nt, tiles, tile_src, tile_dst, leaf_rhs, leaf_inv, leaf_owner, anc_rhs, anc_inv, anc_owner):
    depth, count = leaf_rhs.shape[-2:]
    kinds = tiles.shape[2]
    ch, share, every = depth // n, count // n, n * nt
    waves = WAVES - 1
    phases = 6 + 3 * waves
    any_spec = pl.BlockSpec(memory_space=pl.ANY)
    smem = pl.BlockSpec(memory_space=pltpu.SMEM)
    found = pl.pallas_call(
        functools.partial(kernel, n, nt),
        out_shape=jax.ShapeDtypeStruct((waves * WB, share, depth), BF16),
        in_specs=[any_spec, smem, smem, any_spec, any_spec, smem, any_spec, any_spec, smem],
        out_specs=pl.BlockSpec(memory_space=pltpu.VMEM),
        scratch_shapes=[
            pltpu.VMEM((kinds, depth, depth), BF16),
            pltpu.VMEM((depth, count), BF16),
            pltpu.VMEM((depth, depth), BF16),
            pltpu.VMEM((depth, count), BF16),
            pltpu.VMEM((depth, depth), BF16),
            pltpu.VMEM((n, share, depth), BF16),
            pltpu.VMEM((n, share, depth), BF16),
            pltpu.VMEM((n, WB, share, depth), BF16),
            pltpu.VMEM((n, ch, depth // nt), BF16),
            pltpu.VMEM((waves, ch, depth // nt), BF16),
            pltpu.VMEM((waves, n, ch, depth), BF16),
            pltpu.VMEM((WB * waves, count, depth), BF16),
            pltpu.VMEM((waves, WB, n, share, depth), BF16),
            pltpu.VMEM((waves, every, share, depth), BF16),
            pltpu.VMEM((waves, WB, n, share, depth), BF16),
            pltpu.SemaphoreType.DMA((5,)),
            pltpu.SemaphoreType.DMA((phases,)),
            pltpu.SemaphoreType.DMA((phases,)),
        ],
        compiler_params=pltpu.CompilerParams(collective_id=0, has_side_effects=True),
    )(tiles, tile_src, tile_dst, leaf_rhs, leaf_inv, leaf_owner, anc_rhs, anc_inv, anc_owner)
    return jnp.swapaxes(found, 1, 2)


def solution(mesh):
    n, nt = mesh.shape["rows"], mesh.shape["trees"]
    placed = (
        P("trees", "rows", None, None, None),
        P("trees", "rows", None),
        P("trees", "rows", None),
        P("trees", "rows", None, None),
        P("trees", "rows", None, None),
        P("trees", None),
        P("trees", "rows", None, None),
        P("rows", None, None),
        P(),
    )

    def body(*args):
        depth, count = args[3].shape[-2:]
        if nt == WB and n > 3 and depth % (16 * n) == 0 and depth % (128 * nt) == 0 and count % (8 * n) == 0:
            return fast_body(n, nt, *args)
        return general_body(*args)

    return jax.shard_map(
        body, mesh=mesh, in_specs=placed, out_specs=P(None, None, "rows"), check_vma=False
    )
```
